1024 devices in a mesh: pipe: 16 (over z, x_hi), expert: 64 (over x_lo, y, core).
Axes of the slice: x: 8 (x_hi: 2, x_lo: 4; x = x_hi * 4 + x_lo), y: 8, z: 8, core: 2. Of those that a mesh axis runs over, the one named last changes fastest.
Arguments:
- up_state: bfloat16 [16, 1024, 3584], P('pipe', 'expert'), may hold values from -6 to 6
- down_state: bfloat16 [16, 1024, 3584], P('pipe', 'expert'), may hold values from -6 to 6
- entering_up: bfloat16 [1024, 3584], P('expert'), may hold values from -6 to 6
- entering_down: bfloat16 [1024, 3584], P('expert'), may hold values from -6 to 6
- up_route: int32 [2, 16, 1024, 1], P(None, 'pipe', 'expert'), may hold values from 0 to 7; in each aligned block of 16 rows (0 to 15, 16 to 31, ..., all dimensions but the last counted through in order) at most 2 rows name the same one
- down_route: int32 [2, 16, 1024, 1], P(None, 'pipe', 'expert'), may hold values from 0 to 7; in each aligned block of 16 rows (0 to 15, 16 to 31, ..., all dimensions but the last counted through in order) at most 2 rows name the same one
- norm_gain: float32 [16, 3584], P('pipe'), may hold values from 0.5 to 1.5
- router: bfloat16 [16, 3584, 8], P('pipe'), may hold values from -0.09375 to 0.09375
- w_gate: bfloat16 [16, 3584, 8192], P('pipe', None, 'expert'), may hold values from -0.09375 to 0.09375
- w_up: bfloat16 [16, 3584, 8192], P('pipe', None, 'expert'), may hold values from -0.09375 to 0.09375
- w_down: bfloat16 [16, 8192, 3584], P('pipe', 'expert'), may hold values from -0.1875 to 0.1875
Outputs:
- up_out: bfloat16 [16, 1024, 3584], P('pipe', 'expert')
- down_out: bfloat16 [16, 1024, 3584], P('pipe', 'expert')
The draws below stay inside these ranges and needn't reach their ends.
Inputs may be any that keep to these rules, and one draw needn't show every extreme that they name: `up_route`: each row names one expert. Within each aligned block of 16 rows (the rows of one device) every expert is named by exactly 2 rows. `down_route`: as for up_route.
All inputs are finite; a program needn't handle non-finite values.
Results may differ from the reference program's by a relative error of at most 0.0057.
Values may be sent and summed in bfloat16 or wider, within the bound.
A program may use at most 32 MiB of HBM per device.

```python
import math
import jax
import jax.numpy as jnp
import numpy as np
from jax import lax

D = 3584
FFE = 1024
TOP = 1
TICKS = 2
ROWS = 16
GROUP = 8
EXPERTS = 8
CAP = 2
HID = 128
SECTIONS = 16
RT = 1024
N_EXPERT = 64


def level_of(key, extent, cuts, smallest, high):
    factor_of, own = 1.0, jax.random.fold_in(key, 6)
    for dim, shards_of in cuts:
        steps = jnp.exp(jax.random.uniform(jax.random.fold_in(own, dim), (shards_of,), jnp.float32, smallest / len(cuts), high / len(cuts)))
        factor_of = factor_of * jnp.repeat(steps, extent[dim] // shards_of).reshape([-1 if axis == dim else 1 for axis in range(len(extent))])
    return factor_of


def routed_block(stream_key, own, number, rows, count, top, reach, lean):
    order = jax.random.permutation(stream_key, count)
    crowded, ordinary = load_shares(count, rows * top, reach, lean, True), load_shares(count, rows * top, reach, lean, False)
    places = jnp.arange(count)

    def named(lengths, rotation):
        used = int((lengths > 0).sum())
        fixed = max(1, used // 4)
        shifted = fixed + (places - fixed + rotation * (used - fixed)) % max(1, count - fixed)
        return jnp.zeros((count,), jnp.int32).at[order[jnp.where(places < fixed, places, shifted)]].set(jnp.asarray(lengths, jnp.int32))

    lengths = jnp.where(number % 4 == 0, named(crowded, number // 4), named(ordinary, number - number // 4 - 1))
    mixed = jax.random.permutation(jax.random.fold_in(own, 3), count)
    source_of, sink = mixed[0:count // 2 * 2:2], mixed[1:count // 2 * 2:2]
    room = jnp.minimum(lengths[source_of] - 1, reach - lengths[sink]) // 2
    room = jnp.where((source_of == order[0]) | (sink == order[0]) | (lengths[sink] == 0), 0, jnp.maximum(room, 0))
    shifted = jax.random.randint(jax.random.fold_in(own, 4), (count // 2,), 0, 1 << 20) % (room + 1)
    lengths = lengths.at[source_of].add(-shifted).at[sink].add(shifted)
    members = jnp.searchsorted(jnp.cumsum(lengths), jnp.arange(rows * top), side="right").astype(jnp.int32)
    table = members.reshape(top, rows).T
    table = table[jax.random.permutation(jax.random.fold_in(own, 1), rows)]
    rotation = jax.random.randint(jax.random.fold_in(own, 2), (rows, 1), 0, top)
    return jnp.take_along_axis(table, (jnp.arange(top)[None, :] + rotation) % top, axis=1)


def load_shares(amount, total, bound, skew, full):
    loads = [(1 << 20) // math.isqrt(rank ** skew) + 1 for rank in range(1, amount + 1)]
    largest = bound if full else min(bound, max(-(-total // amount), total * loads[0] // sum(loads)))
    least = 1 if total - largest >= amount - 1 else 0
    holding, spare = [largest] + [least] * (amount - 1), total - largest - least * (amount - 1)
    while spare > 0:
        movable = [i for i in range(1, amount) if holding[i] < largest] or [i for i in range(1, amount) if holding[i] < bound]
        mass, remaining = sum([loads[i] for i in movable]), spare
        for i in movable:
            addition = min(bound - holding[i], max(1, remaining * loads[i] // mass), spare)
            holding[i] = holding[i] + addition
            spare = spare - addition
    return np.array(holding)


def gaussian(key, extent, scale, limit, shards=(), held_as=jnp.bfloat16):
    factor_of = level_of(key, extent, shards, -0.22, 0.18) if shards else 1.0
    drawn = jax.random.normal(key, extent, jnp.float32) * scale * factor_of
    return jnp.minimum(jnp.maximum(drawn, -limit), limit).astype(held_as)


def setup_inputs(seed: int = 0) -> dict:
    key_list = jax.random.split(jax.random.key(seed), 12)
    up_state = gaussian(key_list[0], (SECTIONS, RT, D), 1.0, 6.0, ((0, 16), (1, 64)))
    down_state = gaussian(key_list[1], (SECTIONS, RT, D), 1.0, 6.0, ((0, 16), (1, 64)))
    entering_up = gaussian(key_list[2], (RT, D), 1.0, 6.0, ((0, 64),))
    entering_down = gaussian(key_list[3], (RT, D), 1.0, 6.0, ((0, 64),))
    up_route_keys = jax.random.split(jax.random.fold_in(key_list[4], 1), TICKS * SECTIONS * RT // ROWS)
    up_route_turns = jax.random.permutation(jax.random.fold_in(key_list[4], 3), TICKS * SECTIONS * RT // ROWS)
    up_route = jax.vmap(lambda own, number: routed_block(jax.random.fold_in(key_list[4], 2), own, number, ROWS, EXPERTS, TOP, CAP, 0))(up_route_keys, up_route_turns).reshape((TICKS, SECTIONS, RT, TOP))
    down_route_keys = jax.random.split(jax.random.fold_in(key_list[5], 1), TICKS * SECTIONS * RT // ROWS)
    down_route_turns = jax.random.permutation(jax.random.fold_in(key_list[5], 3), TICKS * SECTIONS * RT // ROWS)
    down_route = jax.vmap(lambda own, number: routed_block(jax.random.fold_in(key_list[5], 2), own, number, ROWS, EXPERTS, TOP, CAP, 0))(down_route_keys, down_route_turns).reshape((TICKS, SECTIONS, RT, TOP))
    norm_gain = jnp.clip(1.0 + 0.1 * jax.random.normal(key_list[6], (SECTIONS, D), jnp.float32), 0.5, 1.5)
    router = gaussian(key_list[7], (SECTIONS, D, EXPERTS), D ** -0.5, 0.09375, ((0, 16),))
    w_gate = gaussian(key_list[8], (SECTIONS, D, EXPERTS * FFE), D ** -0.5, 0.09375, ((0, 16), (2, 64)))
    w_up = gaussian(key_list[9], (SECTIONS, D, EXPERTS * FFE), D ** -0.5, 0.09375, ((0, 16), (2, 64)))
    w_down = gaussian(key_list[10], (SECTIONS, EXPERTS * FFE, D), FFE ** -0.5, 0.1875, ((0, 16), (1, 64)))
    return {"up_state": up_state, "down_state": down_state, "entering_up": entering_up, "entering_down": entering_down, "up_route": up_route, "down_route": down_route, "norm_gain": norm_gain, "router": router, "w_gate": w_gate, "w_up": w_up, "w_down": w_down}


norm_eps = 1e-06

def slot_table(routing):
    blocks = routing.reshape(N_EXPERT, ROWS * TOP)
    onehot = (blocks[:, :, None] == jnp.arange(EXPERTS, dtype=jnp.int32)[None, None, :]).astype(jnp.int32)
    before = jnp.cumsum(onehot, axis=1) - onehot
    slot_ids = lax.optimization_barrier(jnp.sum(before * onehot, axis=2))
    owner_base = jnp.arange(N_EXPERT, dtype=jnp.int32)[:, None] * CAP
    return (slot_ids + owner_base).reshape(RT, TOP).astype(jnp.int32)

def section(token_rows, routing, gain_row, router_cols, gate_cols, up_cols, down_rows):
    widened = token_rows.astype(jnp.float32)
    inverse = lax.rsqrt(lax.optimization_barrier(jnp.mean(widened * widened, axis=1, keepdims=True)) + norm_eps)
    normed = (widened * inverse * gain_row.astype(jnp.float32)).astype(jnp.bfloat16)
    logits = jnp.dot(normed, router_cols, preferred_element_type=jnp.float32)
    affinity = jax.nn.sigmoid(logits)
    weights = jnp.take_along_axis(affinity, routing, axis=1)
    position = slot_table(routing)
    buffer = jnp.zeros((EXPERTS, N_EXPERT * CAP, D), jnp.bfloat16)
    buffer = buffer.at[routing, position].set(jnp.broadcast_to(normed[:, None, :], (RT, TOP, D)))

    def one_expert(expert_id):
        inputs = buffer[expert_id]
        gate_part = lax.dynamic_slice_in_dim(gate_cols, expert_id * FFE, FFE, 1)
        up_part = lax.dynamic_slice_in_dim(up_cols, expert_id * FFE, FFE, 1)
        down_part = lax.dynamic_slice_in_dim(down_rows, expert_id * FFE, FFE, 0)
        gate_pre = jnp.dot(inputs, gate_part, preferred_element_type=jnp.float32)
        up_pre = jnp.dot(inputs, up_part, preferred_element_type=jnp.float32)
        hidden = (jax.nn.silu(gate_pre) * up_pre).astype(jnp.bfloat16)
        summed = jnp.zeros((N_EXPERT * CAP, D), jnp.float32)
        for shard_id in range(GROUP):
            partial_value = jnp.dot(hidden[:, shard_id * HID:(shard_id + 1) * HID], down_part[shard_id * HID:(shard_id + 1) * HID], preferred_element_type=jnp.float32).astype(jnp.bfloat16)
            summed = summed + lax.optimization_barrier(partial_value).astype(jnp.float32)
        return summed
    outputs = lax.map(one_expert, jnp.arange(EXPERTS, dtype=jnp.int32))
    gathered = outputs[routing, position]
    mixed_rows = widened + lax.optimization_barrier(jnp.sum(weights[:, :, None] * gathered, axis=1))
    return mixed_rows.astype(jnp.bfloat16)

def reference(up_state, down_state, entering_up, entering_down, up_route, down_route, norm_gain, router, w_gate, w_up, w_down):

    def apply_section(packed):
        return section(*packed)

    def apply_all(states, routings):
        return lax.map(apply_section, (states, routings, norm_gain, router, w_gate, w_up, w_down))
    up_now = up_state
    down_now = down_state
    up_done = up_state
    down_done = down_state
    for tick_id in range(TICKS):
        up_done = apply_all(up_now, up_route[tick_id])
        down_done = apply_all(down_now, down_route[tick_id])
        if tick_id + 1 < TICKS:
            up_now = jnp.concatenate([entering_up[None], up_done[:-1]], axis=0)
            down_now = jnp.concatenate([down_done[1:], entering_down[None]], axis=0)
    return (up_done, down_done)
```

```python
import functools

import jax
import jax.numpy as jnp
from jax import lax
from jax.experimental import pallas as pl
from jax.experimental.pallas import tpu as pltpu
from jax.sharding import PartitionSpec as P

XS, YS, CORES = 4, 8, 2
HALF = YS // 2
TICKS = 2
ROWS = 16
SLOTS = 8
PARTS = 4
REACH = 5
TRANSIT = 5
norm_eps = 1e-06

MESH = pl.DeviceIdType.MESH
F32, BF16 = jnp.float32, jnp.bfloat16


def iota(shape, dim):
    return lax.broadcasted_iota(jnp.int32, shape, dim)


def turned(row):
    n = row.shape[1]
    eye = iota((n, n), 0) == iota((n, n), 1)
    return jnp.sum(jnp.where(eye, jnp.broadcast_to(row, (n, n)), 0.0), axis=1, keepdims=True)


def slots_of(route, direction):
    n = route.shape[1]
    column = turned(route)
    earlier = iota((n, n), 0) < iota((n, n), 1)
    same = (jnp.broadcast_to(column, (n, n)) == jnp.broadcast_to(route, (n, n))) & earlier
    number = jnp.sum(jnp.where(same, 1.0, 0.0), axis=0, keepdims=True)
    return route * 4.0 + (2.0 * direction) + number


def kernel(
    pipes,
    up_ref, down_ref, enter_up_ref, enter_down_ref, up_route_ref, down_route_ref,
    gain_ref, router_ref, w_gate_ref, w_up_ref, w_down_ref,
    up_out_ref, down_out_ref,
    wgu, wd, normed, xsend, xrecv, away, blocks, pass_on, part, csend, crecv, bsend, brecv, moved_out, moved,
    w_local, w_send, w_recv, x_send, x_recv, y_send, y_recv, c_send, c_recv, b_send, b_recv, m_send, m_recv,
):
    features = up_ref.shape[1]
    width = features // PARTS
    hid = w_down_ref.shape[0]
    pipe = lax.axis_index("pipe")
    place = lax.axis_index("expert")
    core = lax.rem(place, CORES)
    y = lax.rem(place // CORES, YS)
    x = place // (CORES * YS)
    half = y // HALF
    j = lax.rem(y, HALF)

    def at(xx, yy, cc):
        return (pipe, (xx * YS + yy) * CORES + cc)

    def chunk(f):
        return pl.ds(f * width, width)

    def remote(src, dst, send, recv, device):
        return pltpu.make_async_remote_copy(
            src_ref=src, dst_ref=dst, send_sem=send, recv_sem=recv, device_id=device, device_id_type=MESH
        )

    sibling = at(x, y, 1 - core)
    nexts = (at(x, lax.rem(y + 1, YS), core), at(x, lax.rem(y + YS - 1, YS), core))
    ahead = (lax.rem(pipe + 1, pipes), place)
    behind = (lax.rem(pipe + pipes - 1, pipes), place)
    shifts = (ahead, behind)

    def toward(direction, d):
        return lax.rem(y + (d if direction == 0 else YS - d), YS)

    def back(direction, d):
        return toward(1 - direction, d)

    rank = (j, HALF - 1 - j)

    own_weights = [
        pltpu.make_async_copy(w_gate_ref, wgu.at[:, pl.ds(0, hid)], w_local.at[0]),
        pltpu.make_async_copy(w_up_ref, wgu.at[:, pl.ds(2 * hid, hid)], w_local.at[1]),
        pltpu.make_async_copy(w_down_ref, wd.at[pl.ds(0, hid), :], w_local.at[2]),
    ]
    for copy in own_weights:
        copy.start()

    barrier = pltpu.get_barrier_semaphore()
    partners = [at(lax.rem(x + i, XS), y, core) for i in range(1, XS)] + [*nexts, sibling, *shifts]
    for device in partners:
        pl.semaphore_signal(barrier, inc=1, device_id=device, device_id_type=MESH)

    sent = []

    def prepare(t, sources):
        tables = []
        picks = []
        for direction, (source, route_ref) in enumerate(zip(sources, (up_route_ref, down_route_ref))):
            rows = source[...].astype(F32)
            inverse = lax.rsqrt(jnp.mean(rows * rows, axis=1, keepdims=True) + norm_eps)
            normed[direction] = (rows * inverse * gain_ref[...]).astype(BF16)
            route = route_ref[pl.ds(t, 1), :].astype(F32)
            spot = slots_of(route, direction)
            pick = (iota((2 * ROWS, ROWS), 0).astype(F32) == jnp.broadcast_to(spot, (2 * ROWS, ROWS))).astype(BF16)
            picks.append(pick)
            tables.append((route, spot))
        return tables, picks

    def send_rows(t, picks):
        for f in range(PARTS):
            rows = jnp.dot(picks[0], normed[0, :, chunk(f)], preferred_element_type=F32) + jnp.dot(
                picks[1], normed[1, :, chunk(f)], preferred_element_type=F32
            )
            xsend[t, :, :, chunk(f)] = rows.reshape(XS, SLOTS, width).astype(BF16)
        if t == 0:
            pl.semaphore_wait(barrier, len(partners))
        for f in range(PARTS):
            for i in range(1, XS):
                target = lax.rem(x + i, XS)
                copy = remote(
                    xsend.at[t, target, :, chunk(f)], xrecv.at[t, x, :, chunk(f)],
                    x_send.at[t, i - 1, f], x_recv.at[t, i - 1, f], at(target, y, core),
                )
                copy.start()
                sent.append((None, copy))
        xrecv[t, pl.ds(x, 1)] = xsend[t, pl.ds(x, 1)]

    def weigh(t, tables):
        out = []
        for direction, (route, spot) in enumerate(tables):
            logits = lax.dot_general(
                router_ref[...], normed[direction], (((1,), (1,)), ((), ())), preferred_element_type=F32
            )
            affinity = jax.nn.sigmoid(logits)
            count = affinity.shape[0]
            hit = iota((count, ROWS), 0).astype(F32) == jnp.broadcast_to(route, (count, ROWS))
            weight = jnp.sum(jnp.where(hit, affinity, 0.0), axis=0, keepdims=True)
            undo = (iota((ROWS, 2 * ROWS), 1).astype(F32) == jnp.broadcast_to(turned(spot), (ROWS, 2 * ROWS))).astype(BF16)
            out.append((turned(weight), undo))
        return out

    def regroup(back_again):
        a, b = iota((2 * ROWS, 2 * ROWS), 0), iota((2 * ROWS, 2 * ROWS), 1)
        if back_again:
            a, b = b, a
        want = lax.rem(a // 4, XS) * SLOTS + (a // ROWS) * 4 + lax.rem(a, 4)
        return (want == b).astype(BF16)

    def remember(when, copy):
        sent.append((when, copy))

    def guarded(condition, make):
        copy = make()

        @pl.when(condition)
        def _():
            copy.start()

        remember(condition, copy)

    def spread(t):
        forward = regroup(False)
        for f in range(PARTS):
            for i in range(1, XS):
                remote(
                    xsend.at[t, 0, :, chunk(f)], xrecv.at[t, 0, :, chunk(f)],
                    x_send.at[t, i - 1, f], x_recv.at[t, i - 1, f], sibling,
                ).wait_recv()
            rows = xrecv[t, :, :, chunk(f)].astype(F32).reshape(2 * ROWS, width).astype(BF16)
            rows = jnp.dot(forward, rows, preferred_element_type=F32)
            low, high = rows[:ROWS], rows[ROWS:]
            first = half == 0
            blocks[t, pl.ds(y, 1), :, chunk(f)] = jnp.where(first, low, high).astype(BF16)[None]
            away[t, :, chunk(f)] = jnp.where(first, high, low).astype(BF16)
            for r in range(2):
                k = rank[r]
                guarded(k == HALF - 2, lambda: remote(
                    away.at[t, :, chunk(f)], pass_on.at[t, r, :, chunk(f)],
                    y_send.at[t, r, TRANSIT, f], y_recv.at[t, r, TRANSIT, f], nexts[r],
                ))
                guarded(k == HALF - 1, lambda: remote(
                    away.at[t, :, chunk(f)], blocks.at[t, y, :, chunk(f)],
                    y_send.at[t, r, 0, f], y_recv.at[t, r, 0, f], nexts[r],
                ))
            for r in range(2):
                k = rank[r]
                guarded(k < HALF - 1, lambda: remote(
                    blocks.at[t, y, :, chunk(f)], blocks.at[t, y, :, chunk(f)],
                    y_send.at[t, r, 0, f], y_recv.at[t, r, 0, f], nexts[r],
                ))
        for f in range(PARTS):
            for r in range(2):
                k = rank[r]

                @pl.when(k == HALF - 1)
                def _():
                    remote(
                        pass_on.at[t, r, :, chunk(f)], pass_on.at[t, r, :, chunk(f)],
                        y_send.at[t, r, TRANSIT, f], y_recv.at[t, r, TRANSIT, f], nexts[r],
                    ).wait_recv()

                guarded(k == HALF - 1, lambda: remote(
                    pass_on.at[t, r, :, chunk(f)], blocks.at[t, back(r, 1), :, chunk(f)],
                    y_send.at[t, r, 1, f], y_recv.at[t, r, 1, f], nexts[r],
                ))
        for d in range(1, REACH + 1):
            for f in range(PARTS):
                for r in range(2):
                    k = rank[r]
                    slot = back(r, d)

                    @pl.when(d <= k + 2)
                    def _():
                        remote(
                            blocks.at[t, slot, :, chunk(f)], blocks.at[t, slot, :, chunk(f)],
                            y_send.at[t, r, d - 1, f], y_recv.at[t, r, d - 1, f], nexts[r],
                        ).wait_recv()

                    if d < REACH:
                        guarded((k < HALF - 1) & (d <= k + 2), lambda: remote(
                            blocks.at[t, slot, :, chunk(f)], blocks.at[t, slot, :, chunk(f)],
                            y_send.at[t, r, d, f], y_recv.at[t, r, d, f], nexts[r],
                        ))

    def experts(t):
        total = jnp.zeros((YS * ROWS, 4 * hid), F32)
        for f in range(PARTS):
            total = total + jnp.dot(
                blocks[t, :, :, chunk(f)].reshape(YS * ROWS, width), wgu[chunk(f), :], preferred_element_type=F32
            )
        gate, up = total[:, : 2 * hid], total[:, 2 * hid :]
        hidden = (gate / (1.0 + jnp.exp(-gate)) * up).astype(BF16)
        for f in range(PARTS):
            piece = jnp.dot(hidden, wd[:, chunk(f)], preferred_element_type=F32)
            part[:, :, chunk(f)] = piece.reshape(YS, ROWS, width)

    def gather(t):
        for d in range(REACH, 0, -1):
            for f in range(PARTS):
                for r in range(2):
                    k = rank[r]
                    slot = toward(r, d)

                    @pl.when(k == 0)
                    def _():
                        csend[t, r, d - 1, :, chunk(f)] = part[slot, :, chunk(f)].astype(BF16)

                    if d < REACH:

                        @pl.when((k >= 1) & (d <= REACH - k))
                        def _():
                            remote(
                                csend.at[t, r, d - 1, :, chunk(f)], crecv.at[t, r, d, :, chunk(f)],
                                c_send.at[t, r, d - 1, f], c_recv.at[t, r, d, f], nexts[r],
                            ).wait_recv()
                            both = part[slot, :, chunk(f)] + crecv[t, r, d, :, chunk(f)].astype(F32)
                            csend[t, r, d - 1, :, chunk(f)] = both.astype(BF16)

                    guarded((k < HALF - 1) & (d <= REACH - k), lambda: remote(
                        csend.at[t, r, d - 1, :, chunk(f)], crecv.at[t, r, d - 1, :, chunk(f)],
                        c_send.at[t, r, d - 1, f], c_recv.at[t, r, d - 1, f], nexts[r],
                    ))
                    if d <= 2:
                        guarded(k == HALF - 1, lambda: remote(
                            csend.at[t, r, d - 1, :, chunk(f)], crecv.at[t, r, 6 - d, :, chunk(f)],
                            c_send.at[t, r, d - 1, f], c_recv.at[t, r, 6 - d, f], nexts[r],
                        ))

        def arrival(r, slot, f):
            return remote(
                csend.at[t, r, 0, :, chunk(f)], crecv.at[t, r, slot, :, chunk(f)],
                c_send.at[t, r, 0, f], c_recv.at[t, r, slot, f], nexts[r],
            )

        for f in range(PARTS):
            for r in range(2):
                k = rank[r]

                @pl.when(k == 0)
                def _():
                    arrival(r, 4, f).wait_recv()

                guarded(k == 0, lambda: remote(
                    crecv.at[t, r, 4, :, chunk(f)], crecv.at[t, r, TRANSIT, :, chunk(f)],
                    c_send.at[t, r, TRANSIT, f], c_recv.at[t, r, TRANSIT, f], nexts[r],
                ))
        backward = regroup(True)
        for f in range(PARTS):
            for r in range(2):
                k = rank[r]

                @pl.when(k >= 1)
                def _():
                    arrival(r, 0, f).wait_recv()
                    part[pl.ds(y, 1), :, chunk(f)] += crecv[t, r, pl.ds(0, 1), :, chunk(f)].astype(F32)

            for r in range(2):

                @pl.when(rank[r] <= 1)
                def _():
                    arrival(r, TRANSIT, f).wait_recv()

            own = part[pl.ds(y, 1), :, chunk(f)].reshape(ROWS, width)
            other = crecv[t, pl.ds(j // 2, 1), TRANSIT, :, chunk(f)].reshape(ROWS, width).astype(F32)
            first = half == 0
            low, high = jnp.where(first, own, other), jnp.where(first, other, own)
            rows = jnp.concatenate([low, high], axis=0).astype(BF16)
            rows = jnp.dot(backward, rows, preferred_element_type=F32)
            bsend[t, :, :, chunk(f)] = rows.reshape(XS, SLOTS, width).astype(BF16)
            for i in range(1, XS):
                target = lax.rem(x + i, XS)
                copy = remote(
                    bsend.at[t, target, :, chunk(f)], brecv.at[t, x, :, chunk(f)],
                    b_send.at[t, i - 1, f], b_recv.at[t, i - 1, f], at(target, y, core),
                )
                copy.start()
                remember(None, copy)
            brecv[t, pl.ds(x, 1), :, chunk(f)] = bsend[t, pl.ds(x, 1), :, chunk(f)]

    def finish(t, sources, mixes, keep):
        for f in range(PARTS):
            for i in range(1, XS):
                remote(
                    bsend.at[t, 0, :, chunk(f)], brecv.at[t, 0, :, chunk(f)],
                    b_send.at[t, i - 1, f], b_recv.at[t, i - 1, f], sibling,
                ).wait_recv()
            rows = brecv[t, :, :, chunk(f)].astype(F32).reshape(2 * ROWS, width).astype(BF16)
            for direction, (weight, undo) in enumerate(mixes):
                picked = jnp.dot(undo, rows, preferred_element_type=F32)
                result = sources[direction][:, chunk(f)].astype(F32) + weight * picked
                keep(direction, f, result.astype(BF16))

    last = pipes - 1
    edges = (pipe == 0, pipe == last)
    leaves = (pipe < last, pipe > 0)
    entering = (enter_up_ref, enter_down_ref)

    sources = (up_ref, down_ref)
    tables, picks = prepare(0, sources)
    send_rows(0, picks)

    for copy in own_weights:
        copy.wait()
    swaps = [
        (wgu.at[:, pl.ds(0, hid)], wgu.at[:, pl.ds(hid, hid)]),
        (wgu.at[:, pl.ds(2 * hid, hid)], wgu.at[:, pl.ds(3 * hid, hid)]),
        (wd.at[pl.ds(0, hid), :], wd.at[pl.ds(hid, hid), :]),
    ]
    swaps = [remote(src, dst, w_send.at[i], w_recv.at[i], sibling) for i, (src, dst) in enumerate(swaps)]
    for copy in swaps:
        copy.start()
        remember(None, copy)

    mixes = weigh(0, tables)
    spread(0)
    for copy in swaps:
        copy.wait_recv()
    experts(0)
    gather(0)

    def keep_moved(direction, f, value):
        moved_out[direction, :, chunk(f)] = value
        guarded(leaves[direction], lambda: remote(
            moved_out.at[direction, :, chunk(f)], moved.at[direction, :, chunk(f)],
            m_send.at[direction, f], m_recv.at[direction, f], shifts[direction],
        ))

    finish(0, sources, mixes, keep_moved)
    for direction in range(2):

        @pl.when(edges[direction])
        def _():
            moved[direction] = entering[direction][...]

        @pl.when(jnp.logical_not(edges[direction]))
        def _():
            for f in range(PARTS):
                remote(
                    moved_out.at[direction, :, chunk(f)], moved.at[direction, :, chunk(f)],
                    m_send.at[direction, f], m_recv.at[direction, f], shifts[direction],
                ).wait_recv()

    sources = (moved.at[0], moved.at[1])
    tables, picks = prepare(1, sources)
    send_rows(1, picks)
    mixes = weigh(1, tables)
    spread(1)
    experts(1)
    gather(1)

    outs = (up_out_ref, down_out_ref)

    def keep_out(direction, f, value):
        outs[direction][:, chunk(f)] = value

    finish(1, sources, mixes, keep_out)

    for condition, copy in sent:
        if condition is None:
            copy.wait_send()
        else:

            @pl.when(condition)
            def _():
                copy.wait_send()


def shards(pipes, up_state, down_state, enter_up, enter_down, up_route, down_route, gain, router, w_gate, w_up, w_down):
    features = up_state.shape[2]
    hid = w_down.shape[1]
    vmem = pl.BlockSpec(memory_space=pltpu.VMEM)
    hbm = pl.BlockSpec(memory_space=pl.ANY)
    dma = pltpu.SemaphoreType.DMA
    block = jax.ShapeDtypeStruct((ROWS, features), BF16)
    up_out, down_out = pl.pallas_call(
        functools.partial(kernel, pipes),
        out_shape=(block, block),
        in_specs=[vmem] * 8 + [hbm] * 3,
        out_specs=(vmem, vmem),
        scratch_shapes=[
            pltpu.VMEM((features, 4 * hid), BF16),
            pltpu.VMEM((2 * hid, features), BF16),
            pltpu.VMEM((2, ROWS, features), BF16),
            pltpu.VMEM((TICKS, XS, SLOTS, features), BF16),
            pltpu.VMEM((TICKS, XS, SLOTS, features), BF16),
            pltpu.VMEM((TICKS, ROWS, features), BF16),
            pltpu.VMEM((TICKS, YS, ROWS, features), BF16),
            pltpu.VMEM((TICKS, 2, ROWS, features), BF16),
            pltpu.VMEM((YS, ROWS, features), F32),
            pltpu.VMEM((TICKS, 2, REACH, ROWS, features), BF16),
            pltpu.VMEM((TICKS, 2, REACH + 1, ROWS, features), BF16),
            pltpu.VMEM((TICKS, XS, SLOTS, features), BF16),
            pltpu.VMEM((TICKS, XS, SLOTS, features), BF16),
            pltpu.VMEM((2, ROWS, features), BF16),
            pltpu.VMEM((2, ROWS, features), BF16),
            dma((3,)),
            dma((3,)),
            dma((3,)),
            dma((TICKS, XS - 1, PARTS)),
            dma((TICKS, XS - 1, PARTS)),
            dma((TICKS, 2, 6, PARTS)),
            dma((TICKS, 2, 6, PARTS)),
            dma((TICKS, 2, 6, PARTS)),
            dma((TICKS, 2, 6, PARTS)),
            dma((TICKS, XS - 1, PARTS)),
            dma((TICKS, XS - 1, PARTS)),
            dma((2, PARTS)),
            dma((2, PARTS)),
        ],
        compiler_params=pltpu.CompilerParams(
            collective_id=0, has_side_effects=True, vmem_limit_bytes=56 * 1024 * 1024
        ),
    )(
        up_state[0], down_state[0], enter_up, enter_down,
        up_route.reshape(TICKS, ROWS), down_route.reshape(TICKS, ROWS),
        gain, router[0].T, w_gate[0], w_up[0], w_down[0],
    )
    return up_out[None], down_out[None]


def solution(mesh):
    return jax.shard_map(
        functools.partial(shards, mesh.shape["pipe"]),
        mesh=mesh,
        in_specs=(
            P("pipe", "expert", None),
            P("pipe", "expert", None),
            P("expert", None),
            P("expert", None),
            P(None, "pipe", "expert", None),
            P(None, "pipe", "expert", None),
            P("pipe", None),
            P("pipe", None, None),
            P("pipe", None, "expert"),
            P("pipe", None, "expert"),
            P("pipe", "expert", None),
        ),
        out_specs=(P("pipe", "expert", None), P("pipe", "expert", None)),
        check_vma=False,
    )
```

```python
import functools

import jax
import jax.numpy as jnp
from jax import lax
from jax.experimental import pallas as pl
from jax.experimental.pallas import tpu as pltpu
from jax.sharding import PartitionSpec as P

XS, YS, CORES = 4, 8, 2
HALF = YS // 2
TICKS = 2
ROWS = 16
PARTS = 2
SUB = 8
REACH = 5
TRANSIT = 5
norm_eps = 1e-06

MESH = pl.DeviceIdType.MESH
F32, BF16 = jnp.float32, jnp.bfloat16


def iota(shape, dim):
    return lax.broadcasted_iota(jnp.int32, shape, dim)


def turned(row):
    n = row.shape[1]
    eye = iota((n, n), 0) == iota((n, n), 1)
    return jnp.sum(jnp.where(eye, jnp.broadcast_to(row, (n, n)), 0.0), axis=1, keepdims=True)


def slots_of(route):
    n = route.shape[1]
    column = turned(route)
    earlier = iota((n, n), 0) < iota((n, n), 1)
    same = (jnp.broadcast_to(column, (n, n)) == jnp.broadcast_to(route, (n, n))) & earlier
    number = jnp.sum(jnp.where(same, 1.0, 0.0), axis=0, keepdims=True)
    return route * 2.0 + number


def packed(shape, dim):
    i = iota(shape, dim)
    return (i // SUB) * 4 + i % 4, (i // 4) % 2


def kernel(
    pipes,
    up_ref, down_ref, enter_up_ref, enter_down_ref, up_route_ref, down_route_ref,
    gain_ref, router_ref, w_gate_ref, w_up_ref, w_down_ref,
    out_ref,
    wgu, wd, cur, normed, xsend, xrecv, away, blocks, pass_on, part, csend, crecv, bsend, brecv, before, tables_out,
    tables_in, result,
    w_local, w_send, w_recv, in_sem, out_sem, x_send, x_recv, y_send, y_recv, c_send, c_recv, b_send, b_recv,
    m_send, m_recv,
):
    features = up_ref.shape[1]
    width = features // PARTS
    lanes = width // 2
    hid = w_down_ref.shape[0]
    pipe = lax.axis_index("pipe")
    place = lax.axis_index("expert")
    core = lax.rem(place, CORES)
    y = lax.rem(lax.div(place, CORES), YS)
    x = lax.div(place, CORES * YS)
    half = lax.div(y, HALF)
    j = lax.rem(y, HALF)

    def at(xx, yy, cc):
        return (pipe, (xx * YS + yy) * CORES + cc)

    def chunk(f):
        return pl.ds(pl.multiple_of(f * width, 128), width)

    def side(h):
        return pl.ds(h * lanes, lanes)

    def remote(src, dst, send, recv, device):
        return pltpu.make_async_remote_copy(
            src_ref=src, dst_ref=dst, send_sem=send, recv_sem=recv, device_id=device, device_id_type=MESH
        )

    sibling = at(x, y, 1 - core)
    nexts = (at(x, lax.rem(y + 1, YS), core), at(x, lax.rem(y + YS - 1, YS), core))
    columns = [lax.rem(x + i, XS) for i in range(XS)]
    neighbours = (lax.rem(pipe + 1, pipes), lax.rem(pipe + pipes - 1, pipes))
    edges = (pipe == 0, pipe == pipes - 1)
    leaves = (pipe < pipes - 1, pipe > 0)

    def beyond(g, i):
        return (neighbours[g], (columns[i] * YS + y) * CORES + core)

    def toward(r, d):
        return lax.rem(y + (d if r == 0 else YS - d), YS)

    rank = (j, HALF - 1 - j)

    def loads():
        for g, ref in enumerate((up_ref, down_ref)):
            for f in range(PARTS):
                yield pltpu.make_async_copy(ref.at[:, chunk(f)], cur.at[0, g, f], in_sem.at[0, g, f])

    def enters(g):
        ref = (enter_up_ref, enter_down_ref)[g]
        for f in range(PARTS):
            yield pltpu.make_async_copy(ref.at[:, chunk(f)], cur.at[1, g, f], in_sem.at[1, g, f])

    own_weights = [
        pltpu.make_async_copy(w_gate_ref, wgu.at[:, pl.ds(0, hid)], w_local.at[0]),
        pltpu.make_async_copy(w_up_ref, wgu.at[:, pl.ds(2 * hid, hid)], w_local.at[1]),
        pltpu.make_async_copy(w_down_ref, wd.at[pl.ds(0, hid), :], w_local.at[2]),
    ]
    for copy in loads():
        copy.start()
    for copy in own_weights:
        copy.start()
    for g in range(2):

        @pl.when(edges[g])
        def _():
            for copy in enters(g):
                copy.start()

    barrier = pltpu.get_barrier_semaphore()
    partners = [at(columns[i], y, core) for i in range(1, XS)] + [*nexts, sibling]
    partners += [beyond(g, i) for g in range(2) for i in range(XS)]
    for device in partners:
        pl.semaphore_signal(barrier, inc=1, device_id=device, device_id_type=MESH)

    swaps = [
        (wgu.at[:, pl.ds(0, hid)], wgu.at[:, pl.ds(hid, hid)]),
        (wgu.at[:, pl.ds(2 * hid, hid)], wgu.at[:, pl.ds(3 * hid, hid)]),
        (wd.at[pl.ds(0, hid), :], wd.at[pl.ds(hid, hid), :]),
    ]
    swaps = [remote(src, dst, w_send.at[i], w_recv.at[i], sibling) for i, (src, dst) in enumerate(swaps)]

    def x_copy(t, g, i, f):
        return remote(
            xsend.at[t, g, f, columns[i]], xrecv.at[t, g, f, x], x_send.at[t, g, i, f], x_recv.at[t, g, i, f],
            at(columns[i], y, core),
        )

    def b_copy(t, g, i, f):
        device = beyond(g, i) if t == 0 else at(columns[i], y, core)
        return remote(
            bsend.at[t, g, f, columns[i]], brecv.at[t, g, f, x], b_send.at[t, g, i, f], b_recv.at[t, g, i, f], device,
        )

    def y_copy(t, g, r, f, src, dst, slot):
        return remote(src, dst, y_send.at[t, g, r, slot, f], y_recv.at[t, g, r, slot, f], nexts[r])

    def c_copy(t, g, r, f, src, dst, out_slot, in_slot):
        return remote(src, dst, c_send.at[t, g, r, out_slot, f], c_recv.at[t, g, r, in_slot, f], nexts[r])

    def m_copies(g):
        yield remote(cur.at[0, g], before.at[g], m_send.at[g, 0], m_recv.at[g, 0], beyond(g, 0))
        yield remote(tables_out.at[g], tables_in.at[g], m_send.at[g, 1], m_recv.at[g, 1], beyond(g, 0))

    def out_copy(g, f):
        return pltpu.make_async_copy(result.at[g, f], out_ref.at[g, :, chunk(f)], out_sem.at[g, f])

    def spot_of(t, g):
        route = (up_route_ref, down_route_ref)[g][pl.ds(t, 1), :].astype(F32)
        return route, slots_of(route)

    def send_rows(t, g):
        squares = jnp.zeros((ROWS, width), F32)
        for f in range(PARTS):
            rows = cur[t, g, f].astype(F32)
            squares = squares + rows * rows
        scale = lax.rsqrt(jnp.sum(squares, axis=1, keepdims=True) / features + norm_eps)
        _, spot = spot_of(t, g)
        row, lane_half = packed((2 * ROWS, ROWS), 0)
        picks = [
            ((row.astype(F32) == jnp.broadcast_to(spot, (2 * ROWS, ROWS))) & (lane_half == h)).astype(BF16)
            for h in range(2)
        ]
        if (t, g) == (0, 0):
            pl.semaphore_wait(barrier, len(partners))

        @pl.loop(0, PARTS)
        def _(f):
            own = (cur[t, g, f].astype(F32) * scale * gain_ref[:, chunk(f)]).astype(BF16)
            normed[g, f] = own
            rows = jnp.dot(picks[0], own[:, :lanes], preferred_element_type=F32) + jnp.dot(
                picks[1], own[:, lanes:], preferred_element_type=F32
            )
            xsend[t, g, f] = rows.reshape(XS, SUB, lanes).astype(BF16)
            for i in range(1, XS):
                x_copy(t, g, i, f).start()
            xrecv[t, g, f, pl.ds(x, 1)] = xsend[t, g, f, pl.ds(x, 1)]

    kept = {}

    def weigh(t, g):
        route, spot = spot_of(t, g)
        count = router_ref.shape[0]
        logits = jnp.zeros((count, ROWS), F32)
        for f in range(PARTS):
            logits = logits + lax.dot_general(
                router_ref[:, f * width : (f + 1) * width], normed[g, f], (((1,), (1,)), ((), ())),
                preferred_element_type=F32,
            )
        affinity = jax.nn.sigmoid(logits)
        hit = iota((count, ROWS), 0).astype(F32) == jnp.broadcast_to(route, (count, ROWS))
        weight = turned(jnp.sum(jnp.where(hit, affinity, 0.0), axis=0, keepdims=True))
        if t == 0:
            tables_out[g, 0] = jnp.broadcast_to(weight, (ROWS, 128))
            tables_out[g, 1] = jnp.broadcast_to(turned(spot), (ROWS, 128))

            @pl.when(leaves[g])
            def _():
                for copy in m_copies(g):
                    copy.start()
        else:
            kept[g] = (weight, turned(spot))

    def own_blocks(t, g):
        b, a = iota((ROWS, 2 * ROWS), 0), iota((ROWS, 2 * ROWS), 1)
        want = ((b // 2) % XS) * SUB + (b // SUB) * 2 + b % 2
        maps = [(want + 4 * h == a).astype(BF16) for h in range(2)]

        @pl.loop(0, PARTS)
        def _(f):
            for i in range(1, XS):
                x_copy(t, g, i, f).wait_recv()
            rows = xrecv[t, g, f].astype(F32).reshape(2 * ROWS, lanes).astype(BF16)
            first = half == 0
            for h in range(2):
                both = jnp.dot(maps[h], rows, preferred_element_type=F32)
                low, high = both[:SUB], both[SUB:]
                blocks[t, g, f, pl.ds(y, 1), :, side(h)] = jnp.where(first, low, high).astype(BF16)[None]
                away[t, g, f, :, side(h)] = jnp.where(first, high, low).astype(BF16)
            for r in range(2):
                k = rank[r]

                @pl.when(k == HALF - 2)
                def _():
                    y_copy(t, g, r, f, away.at[t, g, f], pass_on.at[t, g, r, f], TRANSIT).start()

                @pl.when(k == HALF - 1)
                def _():
                    y_copy(t, g, r, f, away.at[t, g, f], blocks.at[t, g, f, y], 0).start()

                @pl.when(k < HALF - 1)
                def _():
                    y_copy(t, g, r, f, blocks.at[t, g, f, y], blocks.at[t, g, f, y], 0).start()

    def relay(t, g, d):
        if d == 0:

            @pl.loop(0, PARTS)
            def _(f):
                for r in range(2):

                    @pl.when(rank[r] == HALF - 1)
                    def _():
                        slot = toward(1 - r, 1)
                        y_copy(t, g, r, f, pass_on.at[t, g, r, f], pass_on.at[t, g, r, f], TRANSIT).wait_recv()
                        y_copy(t, g, r, f, pass_on.at[t, g, r, f], blocks.at[t, g, f, slot], 1).start()

            return

        @pl.loop(0, PARTS)
        def _(f):
            for r in range(2):
                k = rank[r]
                slot = toward(1 - r, d)

                @pl.when(d <= k + 2)
                def _():
                    y_copy(t, g, r, f, blocks.at[t, g, f, slot], blocks.at[t, g, f, slot], d - 1).wait_recv()

                if d < REACH:

                    @pl.when((d <= k + 2) & (k < HALF - 1))
                    def _():
                        y_copy(t, g, r, f, blocks.at[t, g, f, slot], blocks.at[t, g, f, slot], d).start()

    def experts(t, g):
        total = jnp.zeros((YS * SUB, 4 * hid), F32)
        for f in range(PARTS):
            total = total + jnp.dot(
                blocks[t, g, f].astype(F32).reshape(YS * SUB, width).astype(BF16),
                wgu[f * width : (f + 1) * width, :],
                preferred_element_type=F32,
            )
        gate, up = total[:, : 2 * hid], total[:, 2 * hid :]
        hidden = (gate / (1.0 + jnp.exp(-gate)) * up).astype(BF16)
        for f in range(PARTS):
            piece = jnp.dot(hidden, wd[:, f * width : (f + 1) * width], preferred_element_type=F32)
            part[g, f] = piece.reshape(YS, SUB, width)

    def arrival(t, g, r, slot, f):
        return c_copy(t, g, r, f, csend.at[t, g, r, f, 0], crecv.at[t, g, r, f, slot], 0, slot)

    def gather(t, g, d):
        if d == 0:

            @pl.loop(0, PARTS)
            def _(f):
                for r in range(2):

                    @pl.when(rank[r] == 0)
                    def _():
                        arrival(t, g, r, 4, f).wait_recv()
                        c_copy(
                            t, g, r, f, crecv.at[t, g, r, f, 4], crecv.at[t, g, r, f, TRANSIT], TRANSIT, TRANSIT
                        ).start()

            return

        @pl.loop(0, PARTS)
        def _(f):
            for r in range(2):
                k = rank[r]
                slot = toward(r, d)

                @pl.when(k == 0)
                def _():
                    csend[t, g, r, f, d - 1] = part[g, f, pl.ds(slot, 1)].reshape(SUB, width).astype(BF16)

                if d < REACH:

                    @pl.when((k >= 1) & (d <= REACH - k))
                    def _():
                        arrival(t, g, r, d, f).wait_recv()
                        both = part[g, f, pl.ds(slot, 1)].reshape(SUB, width) + crecv[t, g, r, f, d].astype(F32)
                        csend[t, g, r, f, d - 1] = both.astype(BF16)

                @pl.when((d <= REACH - k) & (k < HALF - 1))
                def _():
                    c_copy(
                        t, g, r, f, csend.at[t, g, r, f, d - 1], crecv.at[t, g, r, f, d - 1], d - 1, d - 1
                    ).start()

                if d <= 2:

                    @pl.when(k == HALF - 1)
                    def _():
                        c_copy(
                            t, g, r, f, csend.at[t, g, r, f, d - 1], crecv.at[t, g, r, f, 6 - d], d - 1, 6 - d
                        ).start()

    def send_back(t, g):
        a, b = iota((2 * ROWS, ROWS), 0), iota((2 * ROWS, ROWS), 1)
        want = ((b // 2) % XS) * SUB + (b // SUB) * 2 + b % 2
        maps = [(want + 4 * h == a).astype(BF16) for h in range(2)]

        @pl.loop(0, PARTS)
        def _(f):
            for r in range(2):

                @pl.when(rank[r] >= 1)
                def _():
                    arrival(t, g, r, 0, f).wait_recv()
                    part[g, f, pl.ds(y, 1)] += crecv[t, g, r, f, pl.ds(0, 1)].astype(F32)

            for r in range(2):

                @pl.when(rank[r] <= 1)
                def _():
                    arrival(t, g, r, TRANSIT, f).wait_recv()

            own = part[g, f, pl.ds(y, 1)].reshape(SUB, width)
            other = crecv[t, g, pl.ds(lax.div(j, 2), 1), f, TRANSIT].reshape(SUB, width).astype(F32)
            first = half == 0
            rows = jnp.concatenate([jnp.where(first, own, other), jnp.where(first, other, own)], axis=0).astype(BF16)
            rows = jnp.dot(maps[0], rows[:, :lanes], preferred_element_type=F32) + jnp.dot(
                maps[1], rows[:, lanes:], preferred_element_type=F32
            )
            bsend[t, g, f] = rows.reshape(XS, SUB, lanes).astype(BF16)
            if t == 0:

                @pl.when(leaves[g])
                def _():
                    for i in range(XS):
                        b_copy(t, g, i, f).start()
            else:
                for i in range(1, XS):
                    b_copy(t, g, i, f).start()
                brecv[t, g, f, pl.ds(x, 1)] = bsend[t, g, f, pl.ds(x, 1)]

    def settle(t, g):
        row, lane_half = packed((ROWS, 2 * ROWS), 1)

        def mixed(weight, spot, keep, rows_of):
            undo = [
                ((row.astype(F32) == jnp.broadcast_to(spot, (ROWS, 2 * ROWS))) & (lane_half == h)).astype(BF16)
                for h in range(2)
            ]

            @pl.loop(0, PARTS)
            def _(f):
                for i in range(0 if t == 0 else 1, XS):
                    b_copy(t, g, i, f).wait_recv()
                rows = brecv[t, g, f].astype(F32).reshape(2 * ROWS, lanes).astype(BF16)
                for h in range(2):
                    picked = jnp.dot(undo[h], rows, preferred_element_type=F32)
                    keep(f, h, (rows_of(f, h).astype(F32) + weight * picked).astype(BF16))

        if t == 0:

            @pl.when(edges[g])
            def _():
                for copy in enters(g):
                    copy.wait()

            @pl.when(jnp.logical_not(edges[g]))
            def _():
                for copy in m_copies(g):
                    copy.wait_recv()

                def keep(f, h, value):
                    cur[1, g, f, :, side(h)] = value

                mixed(
                    tables_in[g, 0][:, :1], tables_in[g, 1][:, :1], keep, lambda f, h: before[g, f, :, side(h)]
                )

        else:

            def keep(f, h, value):
                result[g, f, :, side(h)] = value

            mixed(*kept[g], keep, lambda f, h: cur[1, g, f, :, side(h)])
            for f in range(PARTS):
                out_copy(g, f).start()

    def start_swaps():
        for copy in own_weights:
            copy.wait()
        for copy in swaps:
            copy.start()

    def end_swaps():
        for copy in swaps:
            copy.wait_recv()

    for copy in loads():
        copy.wait()

    def both(task, *rest):
        for g in range(2):
            task(rest[0], g, *rest[1:])

    for t in range(TICKS):
        both(send_rows, t)
        if t == 0:
            start_swaps()
        both(own_blocks, t)
        for d in range(REACH + 1):
            both(relay, t, d)
        if t == 0:
            end_swaps()
        both(experts, t)
        for d in range(REACH, -1, -1):
            both(gather, t, d)
            if d == REACH:
                both(weigh, t)
        both(send_back, t)
        both(settle, t)

    for copy in swaps:
        copy.wait_send()
    for g in range(2):

        @pl.when(leaves[g])
        def _():
            for copy in m_copies(g):
                copy.wait_send()

            @pl.loop(0, PARTS)
            def _(f):
                for i in range(XS):
                    b_copy(0, g, i, f).wait_send()

    @pl.loop(0, 2)
    def _(g):
        @pl.loop(0, PARTS)
        def _(f):
            for i in range(1, XS):
                remote(
                    bsend.at[1, g, f, 0], brecv.at[1, g, f, 0], b_send.at[1, g, i, f], b_recv.at[1, g, i, f], sibling
                ).wait_send()

            @pl.loop(0, TICKS)
            def _(t):
                for i in range(1, XS):
                    x_copy(t, g, i, f).wait_send()
                for r in range(2):
                    k = rank[r]

                    @pl.loop(0, TRANSIT + 1)
                    def _(slot):
                        spreads = jnp.where(k == HALF - 1, slot <= 1, (slot <= k + 2) & (slot < TRANSIT))

                        @pl.when(spreads | ((slot == TRANSIT) & (k == HALF - 2)))
                        def _():
                            y_copy(t, g, r, f, away.at[t, g, f], pass_on.at[t, g, r, f], slot).wait_send()

                        @pl.when((slot < REACH - k) | ((slot == TRANSIT) & (k == 0)))
                        def _():
                            c_copy(
                                t, g, r, f, csend.at[t, g, r, f, 0], crecv.at[t, g, r, f, 0], slot, 0
                            ).wait_send()

    for g in range(2):
        for f in range(PARTS):
            out_copy(g, f).wait()


def shards(pipes, up_state, down_state, enter_up, enter_down, up_route, down_route, gain, router, w_gate, w_up, w_down):
    features = up_state.shape[2]
    hid = w_down.shape[1]
    vmem = pl.BlockSpec(memory_space=pltpu.VMEM)
    hbm = pl.BlockSpec(memory_space=pl.ANY)
    dma = pltpu.SemaphoreType.DMA
    width = features // PARTS
    out = pl.pallas_call(
        functools.partial(kernel, pipes),
        out_shape=jax.ShapeDtypeStruct((2, ROWS, features), BF16),
        in_specs=[hbm] * 4 + [vmem] * 4 + [hbm] * 3,
        out_specs=hbm,
        scratch_shapes=[
            pltpu.VMEM((features, 4 * hid), BF16),
            pltpu.VMEM((2 * hid, features), BF16),
            pltpu.VMEM((TICKS, 2, PARTS, ROWS, width), BF16),
            pltpu.VMEM((2, PARTS, ROWS, width), BF16),
            pltpu.VMEM((TICKS, 2, PARTS, XS, SUB, width // 2), BF16),
            pltpu.VMEM((TICKS, 2, PARTS, XS, SUB, width // 2), BF16),
            pltpu.VMEM((TICKS, 2, PARTS, SUB, width), BF16),
            pltpu.VMEM((TICKS, 2, PARTS, YS, SUB, width), BF16),
            pltpu.VMEM((TICKS, 2, 2, PARTS, SUB, width), BF16),
            pltpu.VMEM((2, PARTS, YS, SUB, width), F32),
            pltpu.VMEM((TICKS, 2, 2, PARTS, REACH, SUB, width), BF16),
            pltpu.VMEM((TICKS, 2, 2, PARTS, REACH + 1, SUB, width), BF16),
            pltpu.VMEM((TICKS, 2, PARTS, XS, SUB, width // 2), BF16),
            pltpu.VMEM((TICKS, 2, PARTS, XS, SUB, width // 2), BF16),
            pltpu.VMEM((2, PARTS, ROWS, width), BF16),
            pltpu.VMEM((2, 2, ROWS, 128), F32),
            pltpu.VMEM((2, 2, ROWS, 128), F32),
            pltpu.VMEM((2, PARTS, ROWS, width), BF16),
            dma((3,)),
            dma((3,)),
            dma((3,)),
            dma((2, 2, PARTS)),
            dma((2, PARTS)),
            dma((TICKS, 2, XS, PARTS)),
            dma((TICKS, 2, XS, PARTS)),
            dma((TICKS, 2, 2, TRANSIT + 1, PARTS)),
            dma((TICKS, 2, 2, TRANSIT + 1, PARTS)),
            dma((TICKS, 2, 2, TRANSIT + 1, PARTS)),
            dma((TICKS, 2, 2, TRANSIT + 1, PARTS)),
            dma((TICKS, 2, XS, PARTS)),
            dma((TICKS, 2, XS, PARTS)),
            dma((2, 2)),
            dma((2, 2)),
        ],
        compiler_params=pltpu.CompilerParams(
            collective_id=0, has_side_effects=True, vmem_limit_bytes=56 * 1024 * 1024
        ),
    )(
        up_state[0], down_state[0], enter_up, enter_down,
        up_route.reshape(TICKS, ROWS), down_route.reshape(TICKS, ROWS),
        gain, router[0].T, w_gate[0], w_up[0], w_down[0],
    )
    return out[:1], out[1:]


def solution(mesh):
    return jax.shard_map(
        functools.partial(shards, mesh.shape["pipe"]),
        mesh=mesh,
        in_specs=(
            P("pipe", "expert", None),
            P("pipe", "expert", None),
            P("expert", None),
            P("expert", None),
            P(None, "pipe", "expert", None),
            P(None, "pipe", "expert", None),
            P("pipe", None),
            P("pipe", None, None),
            P("pipe", None, "expert"),
            P("pipe", None, "expert"),
            P("pipe", "expert", None),
        ),
        out_specs=(P("pipe", "expert", None), P("pipe", "expert", None)),
        check_vma=False,
    )
```

```python
import functools

import jax
import jax.numpy as jnp
from jax import lax
from jax.experimental import pallas as pl
from jax.experimental.pallas import tpu as pltpu
from jax.sharding import PartitionSpec as P

XS, YS, CORES = 4, 8, 2
HALF = YS // 2
TICKS = 2
ROWS = 16
PARTS = 2
SUB = 8
REACH = 5
TRANSIT = 5
norm_eps = 1e-06

MESH = pl.DeviceIdType.MESH
F32, BF16 = jnp.float32, jnp.bfloat16


def iota(shape, dim):
    return lax.broadcasted_iota(jnp.int32, shape, dim)


def turned(row):
    n = row.shape[1]
    eye = iota((n, n), 0) == iota((n, n), 1)
    return jnp.sum(jnp.where(eye, jnp.broadcast_to(row, (n, n)), 0.0), axis=1, keepdims=True)


def slots_of(route):
    n = route.shape[1]
    column = turned(route)
    earlier = iota((n, n), 0) < iota((n, n), 1)
    same = (jnp.broadcast_to(column, (n, n)) == jnp.broadcast_to(route, (n, n))) & earlier
    number = jnp.sum(jnp.where(same, 1.0, 0.0), axis=0, keepdims=True)
    return route * 2.0 + number


def packed(shape, dim):
    i = iota(shape, dim)
    return (i // SUB) * 4 + i % 4, (i // 4) % 2


def kernel(
    pipes,
    up_ref, down_ref, enter_up_ref, enter_down_ref, up_route_ref, down_route_ref,
    gain_ref, router_ref, w_gate_ref, w_up_ref, w_down_ref,
    out_ref,
    wgu, wd, cur, normed, xsend, xrecv, away, blocks, pass_on, part, csend, crecv, bsend, brecv, before, tables_out,
    tables_in, result,
    w_local, w_send, w_recv, in_sem, out_sem, x_send, x_recv, y_send, y_recv, c_send, c_recv, b_send, b_recv,
    m_send, m_recv,
):
    features = up_ref.shape[1]
    width = features // PARTS
    lanes = width // 2
    hid = w_down_ref.shape[0]
    pipe = lax.axis_index("pipe")
    place = lax.axis_index("expert")
    core = lax.rem(place, CORES)
    y = lax.rem(lax.div(place, CORES), YS)
    x = lax.div(place, CORES * YS)
    half = lax.div(y, HALF)
    j = lax.rem(y, HALF)

    def at(xx, yy, cc):
        return (pipe, (xx * YS + yy) * CORES + cc)

    def chunk(f):
        return pl.ds(pl.multiple_of(f * width, 128), width)

    def side(h):
        return pl.ds(h * lanes, lanes)

    def remote(src, dst, send, recv, device):
        return pltpu.make_async_remote_copy(
            src_ref=src, dst_ref=dst, send_sem=send, recv_sem=recv, device_id=device, device_id_type=MESH
        )

    sibling = at(x, y, 1 - core)
    nexts = (at(x, lax.rem(y + 1, YS), core), at(x, lax.rem(y + YS - 1, YS), core))
    columns = [lax.rem(x + i, XS) for i in range(XS)]
    neighbours = (lax.rem(pipe + 1, pipes), lax.rem(pipe + pipes - 1, pipes))
    edges = (pipe == 0, pipe == pipes - 1)
    leaves = (pipe < pipes - 1, pipe > 0)

    def beyond(g, i):
        return (neighbours[g], (columns[i] * YS + y) * CORES + core)

    def toward(r, d):
        return lax.rem(y + (d if r == 0 else YS - d), YS)

    rank = (j, HALF - 1 - j)

    def loads():
        for g, ref in enumerate((up_ref, down_ref)):
            for f in range(PARTS):
                yield pltpu.make_async_copy(ref.at[:, chunk(f)], cur.at[0, g, f], in_sem.at[0, g, f])

    def enters(g):
        ref = (enter_up_ref, enter_down_ref)[g]
        for f in range(PARTS):
            yield pltpu.make_async_copy(ref.at[:, chunk(f)], cur.at[1, g, f], in_sem.at[1, g, f])

    own_weights = [
        pltpu.make_async_copy(w_gate_ref, wgu.at[:, pl.ds(0, hid)], w_local.at[0]),
        pltpu.make_async_copy(w_up_ref, wgu.at[:, pl.ds(2 * hid, hid)], w_local.at[1]),
        pltpu.make_async_copy(w_down_ref, wd.at[pl.ds(0, hid), :], w_local.at[2]),
    ]
    for copy in loads():
        copy.start()
    for copy in own_weights:
        copy.start()
    for g in range(2):

        @pl.when(edges[g])
        def _():
            for copy in enters(g):
                copy.start()

    barrier = pltpu.get_barrier_semaphore()
    partners = [at(columns[i], y, core) for i in range(1, XS)] + [*nexts, sibling]
    partners += [beyond(g, i) for g in range(2) for i in range(XS)]
    for device in partners:
        pl.semaphore_signal(barrier, inc=1, device_id=device, device_id_type=MESH)

    swaps = [
        (wgu.at[:, pl.ds(0, hid)], wgu.at[:, pl.ds(hid, hid)]),
        (wgu.at[:, pl.ds(2 * hid, hid)], wgu.at[:, pl.ds(3 * hid, hid)]),
        (wd.at[pl.ds(0, hid), :], wd.at[pl.ds(hid, hid), :]),
    ]
    swaps = [remote(src, dst, w_send.at[i], w_recv.at[i], sibling) for i, (src, dst) in enumerate(swaps)]

    def x_copy(t, g, i, f):
        return remote(
            xsend.at[t, g, f, columns[i]], xrecv.at[t, g, f, x], x_send.at[t, g, i, f], x_recv.at[t, g, i, f],
            at(columns[i], y, core),
        )

    def b_copy(t, g, i, f):
        device = beyond(g, i) if t == 0 else at(columns[i], y, core)
        return remote(
            bsend.at[t, g, f, columns[i]], brecv.at[t, g, f, x], b_send.at[t, g, i, f], b_recv.at[t, g, i, f], device,
        )

    def y_copy(t, g, r, f, src, dst, slot):
        return remote(src, dst, y_send.at[t, g, r, slot, f], y_recv.at[t, g, r, slot, f], nexts[r])

    def c_copy(t, g, r, f, src, dst, out_slot, in_slot):
        return remote(src, dst, c_send.at[t, g, r, out_slot, f], c_recv.at[t, g, r, in_slot, f], nexts[r])

    def m_copies(g):
        yield remote(cur.at[0, g], before.at[g], m_send.at[g, 0], m_recv.at[g, 0], beyond(g, 0))
        yield remote(tables_out.at[g], tables_in.at[g], m_send.at[g, 1], m_recv.at[g, 1], beyond(g, 0))

    def out_copy(g, f):
        return pltpu.make_async_copy(result.at[g, f], out_ref.at[g, :, chunk(f)], out_sem.at[g, f])

    def spot_of(t, g):
        route = (up_route_ref, down_route_ref)[g][pl.ds(t, 1), :].astype(F32)
        return route, slots_of(route)

    def send_rows(t, g):
        squares = jnp.zeros((ROWS, width), F32)
        for f in range(PARTS):
            rows = cur[t, g, f].astype(F32)
            squares = squares + rows * rows
        scale = lax.rsqrt(jnp.sum(squares, axis=1, keepdims=True) / features + norm_eps)
        _, spot = spot_of(t, g)
        row, lane_half = packed((2 * ROWS, ROWS), 0)
        picks = [
            ((row.astype(F32) == jnp.broadcast_to(spot, (2 * ROWS, ROWS))) & (lane_half == h)).astype(BF16)
            for h in range(2)
        ]
        if (t, g) == (0, 0):
            pl.semaphore_wait(barrier, len(partners))

        @pl.loop(0, PARTS)
        def _(f):
            own = (cur[t, g, f].astype(F32) * scale * gain_ref[:, chunk(f)]).astype(BF16)
            normed[g, f] = own
            rows = jnp.dot(picks[0], own[:, :lanes], preferred_element_type=F32) + jnp.dot(
                picks[1], own[:, lanes:], preferred_element_type=F32
            )
            xsend[t, g, f] = rows.reshape(XS, SUB, lanes).astype(BF16)
            for i in range(1, XS):
                x_copy(t, g, i, f).start()
            xrecv[t, g, f, pl.ds(x, 1)] = xsend[t, g, f, pl.ds(x, 1)]

    kept = {}

    def weigh(t, g):
        route, spot = spot_of(t, g)
        count = router_ref.shape[0]
        logits = jnp.zeros((count, ROWS), F32)
        for f in range(PARTS):
            logits = logits + lax.dot_general(
                router_ref[:, f * width : (f + 1) * width], normed[g, f], (((1,), (1,)), ((), ())),
                preferred_element_type=F32,
            )
        affinity = jax.nn.sigmoid(logits)
        hit = iota((count, ROWS), 0).astype(F32) == jnp.broadcast_to(route, (count, ROWS))
        weight = turned(jnp.sum(jnp.where(hit, affinity, 0.0), axis=0, keepdims=True))
        if t == 0:
            tables_out[g, 0] = jnp.broadcast_to(weight, (ROWS, 128))
            tables_out[g, 1] = jnp.broadcast_to(turned(spot), (ROWS, 128))

            @pl.when(leaves[g])
            def _():
                for copy in m_copies(g):
                    copy.start()
        else:
            kept[g] = (weight, turned(spot))

    def own_blocks(t, g):
        b, a = iota((ROWS, 2 * ROWS), 0), iota((ROWS, 2 * ROWS), 1)
        want = ((b // 2) % XS) * SUB + (b // SUB) * 2 + b % 2
        maps = [(want + 4 * h == a).astype(BF16) for h in range(2)]

        @pl.loop(0, PARTS)
        def _(f):
            for i in range(1, XS):
                x_copy(t, g, i, f).wait_recv()
            rows = xrecv[t, g, f].astype(F32).reshape(2 * ROWS, lanes).astype(BF16)
            first = half == 0
            for h in range(2):
                both = jnp.dot(maps[h], rows, preferred_element_type=F32)
                low, high = both[:SUB], both[SUB:]
                blocks[t, g, f, pl.ds(y, 1), :, side(h)] = jnp.where(first, low, high).astype(BF16)[None]
                away[t, g, f, :, side(h)] = jnp.where(first, high, low).astype(BF16)
            for r in range(2):
                k = rank[r]

                @pl.when(k == HALF - 2)
                def _():
                    y_copy(t, g, r, f, away.at[t, g, f], pass_on.at[t, g, r, f], TRANSIT).start()

                @pl.when(k == HALF - 1)
                def _():
                    y_copy(t, g, r, f, away.at[t, g, f], blocks.at[t, g, f, y], 0).start()

                @pl.when(k < HALF - 1)
                def _():
                    y_copy(t, g, r, f, blocks.at[t, g, f, y], blocks.at[t, g, f, y], 0).start()

    def relay(t, g, d):
        if d == 0:

            @pl.loop(0, PARTS)
            def _(f):
                for r in range(2):

                    @pl.when(rank[r] == HALF - 1)
                    def _():
                        slot = toward(1 - r, 1)
                        y_copy(t, g, r, f, pass_on.at[t, g, r, f], pass_on.at[t, g, r, f], TRANSIT).wait_recv()
                        y_copy(t, g, r, f, pass_on.at[t, g, r, f], blocks.at[t, g, f, slot], 1).start()

            return

        @pl.loop(0, PARTS)
        def _(f):
            for r in range(2):
                k = rank[r]
                slot = toward(1 - r, d)

                @pl.when(d <= k + 2)
                def _():
                    y_copy(t, g, r, f, blocks.at[t, g, f, slot], blocks.at[t, g, f, slot], d - 1).wait_recv()

                if d < REACH:

                    @pl.when((d <= k + 2) & (k < HALF - 1))
                    def _():
                        y_copy(t, g, r, f, blocks.at[t, g, f, slot], blocks.at[t, g, f, slot], d).start()

    def experts(t):
        count = YS * SUB
        total = jnp.zeros((2 * count, 4 * hid), F32)
        for f in range(PARTS):
            rows = [blocks[t, g, f].astype(F32).reshape(count, width) for g in range(2)]
            total = total + jnp.dot(
                jnp.concatenate(rows, axis=0).astype(BF16), wgu[f * width : (f + 1) * width, :],
                preferred_element_type=F32,
            )
        gate, up = total[:, : 2 * hid], total[:, 2 * hid :]
        hidden = (gate / (1.0 + jnp.exp(-gate)) * up).astype(BF16)
        for f in range(PARTS):
            piece = jnp.dot(hidden, wd[:, f * width : (f + 1) * width], preferred_element_type=F32)
            for g in range(2):
                part[g, f] = piece[g * count : (g + 1) * count].reshape(YS, SUB, width)

    def arrival(t, g, r, slot, f):
        return c_copy(t, g, r, f, csend.at[t, g, r, f, 0], crecv.at[t, g, r, f, slot], 0, slot)

    def gather(t, g, d):
        if d == 0:

            @pl.loop(0, PARTS)
            def _(f):
                for r in range(2):

                    @pl.when(rank[r] == 0)
                    def _():
                        arrival(t, g, r, 4, f).wait_recv()
                        c_copy(
                            t, g, r, f, crecv.at[t, g, r, f, 4], crecv.at[t, g, r, f, TRANSIT], TRANSIT, TRANSIT
                        ).start()

            return

        @pl.loop(0, PARTS)
        def _(f):
            for r in range(2):
                k = rank[r]
                slot = toward(r, d)

                @pl.when(k == 0)
                def _():
                    csend[t, g, r, f, d - 1] = part[g, f, pl.ds(slot, 1)].reshape(SUB, width).astype(BF16)

                if d < REACH:

                    @pl.when((k >= 1) & (d <= REACH - k))
                    def _():
                        arrival(t, g, r, d, f).wait_recv()
                        both = part[g, f, pl.ds(slot, 1)].reshape(SUB, width) + crecv[t, g, r, f, d].astype(F32)
                        csend[t, g, r, f, d - 1] = both.astype(BF16)

                @pl.when((d <= REACH - k) & (k < HALF - 1))
                def _():
                    c_copy(
                        t, g, r, f, csend.at[t, g, r, f, d - 1], crecv.at[t, g, r, f, d - 1], d - 1, d - 1
                    ).start()

                if d <= 2:

                    @pl.when(k == HALF - 1)
                    def _():
                        c_copy(
                            t, g, r, f, csend.at[t, g, r, f, d - 1], crecv.at[t, g, r, f, 6 - d], d - 1, 6 - d
                        ).start()

    def send_back(t, g):
        a, b = iota((2 * ROWS, ROWS), 0), iota((2 * ROWS, ROWS), 1)
        want = ((b // 2) % XS) * SUB + (b // SUB) * 2 + b % 2
        maps = [(want + 4 * h == a).astype(BF16) for h in range(2)]

        @pl.loop(0, PARTS)
        def _(f):
            for r in range(2):

                @pl.when(rank[r] >= 1)
                def _():
                    arrival(t, g, r, 0, f).wait_recv()
                    part[g, f, pl.ds(y, 1)] += crecv[t, g, r, f, pl.ds(0, 1)].astype(F32)

            for r in range(2):

                @pl.when(rank[r] <= 1)
                def _():
                    arrival(t, g, r, TRANSIT, f).wait_recv()

            own = part[g, f, pl.ds(y, 1)].reshape(SUB, width)
            other = crecv[t, g, pl.ds(lax.div(j, 2), 1), f, TRANSIT].reshape(SUB, width).astype(F32)
            first = half == 0
            rows = jnp.concatenate([jnp.where(first, own, other), jnp.where(first, other, own)], axis=0).astype(BF16)
            rows = jnp.dot(maps[0], rows[:, :lanes], preferred_element_type=F32) + jnp.dot(
                maps[1], rows[:, lanes:], preferred_element_type=F32
            )
            bsend[t, g, f] = rows.reshape(XS, SUB, lanes).astype(BF16)
            if t == 0:

                @pl.when(leaves[g])
                def _():
                    for i in range(XS):
                        b_copy(t, g, i, f).start()
            else:
                for i in range(1, XS):
                    b_copy(t, g, i, f).start()
                brecv[t, g, f, pl.ds(x, 1)] = bsend[t, g, f, pl.ds(x, 1)]

    def settle(t, g):
        row, lane_half = packed((ROWS, 2 * ROWS), 1)

        def mixed(weight, spot, keep, rows_of):
            undo = [
                ((row.astype(F32) == jnp.broadcast_to(spot, (ROWS, 2 * ROWS))) & (lane_half == h)).astype(BF16)
                for h in range(2)
            ]

            @pl.loop(0, PARTS)
            def _(f):
                for i in range(0 if t == 0 else 1, XS):
                    b_copy(t, g, i, f).wait_recv()
                rows = brecv[t, g, f].astype(F32).reshape(2 * ROWS, lanes).astype(BF16)
                for h in range(2):
                    picked = jnp.dot(undo[h], rows, preferred_element_type=F32)
                    keep(f, h, (rows_of(f, h).astype(F32) + weight * picked).astype(BF16))

        if t == 0:

            @pl.when(edges[g])
            def _():
                for copy in enters(g):
                    copy.wait()

            @pl.when(jnp.logical_not(edges[g]))
            def _():
                for copy in m_copies(g):
                    copy.wait_recv()

                def keep(f, h, value):
                    cur[1, g, f, :, side(h)] = value

                mixed(
                    tables_in[g, 0][:, :1], tables_in[g, 1][:, :1], keep, lambda f, h: before[g, f, :, side(h)]
                )

        else:

            def keep(f, h, value):
                result[g, f, :, side(h)] = value

            mixed(*kept[g], keep, lambda f, h: cur[1, g, f, :, side(h)])
            for f in range(PARTS):
                out_copy(g, f).start()

    def start_swaps():
        for copy in own_weights:
            copy.wait()
        for copy in swaps:
            copy.start()

    def end_swaps():
        for copy in swaps:
            copy.wait_recv()

    for copy in loads():
        copy.wait()

    def drain():
        for copy in swaps:
            copy.wait_send()
        for g in range(2):

            @pl.when(leaves[g])
            def _():
                for copy in m_copies(g):
                    copy.wait_send()

                @pl.loop(0, PARTS)
                def _(f):
                    for i in range(XS):
                        b_copy(0, g, i, f).wait_send()

        @pl.loop(0, 2)
        def _(g):
            @pl.loop(0, PARTS)
            def _(f):
                @pl.loop(0, TICKS)
                def _(t):
                    for i in range(1, XS):
                        x_copy(t, g, i, f).wait_send()
                    for r in range(2):
                        k = rank[r]

                        @pl.loop(0, TRANSIT + 1)
                        def _(slot):
                            spreads = jnp.where(k == HALF - 1, slot <= 1, (slot <= k + 2) & (slot < TRANSIT))

                            @pl.when(spreads | ((slot == TRANSIT) & (k == HALF - 2)))
                            def _():
                                y_copy(t, g, r, f, away.at[t, g, f], pass_on.at[t, g, r, f], slot).wait_send()

                            @pl.when((slot < REACH - k) | ((slot == TRANSIT) & (k == 0)))
                            def _():
                                c_copy(
                                    t, g, r, f, csend.at[t, g, r, f, 0], crecv.at[t, g, r, f, 0], slot, 0
                                ).wait_send()

    def both(task, *rest):
        for g in range(2):
            task(rest[0], g, *rest[1:])

    for t in range(TICKS):
        both(send_rows, t)
        if t == 0:
            start_swaps()
        both(own_blocks, t)
        for d in range(REACH + 1):
            both(relay, t, d)
        if t == 0:
            end_swaps()
        experts(t)
        for d in range(REACH, -1, -1):
            both(gather, t, d)
            if d == REACH:
                both(weigh, t)
        both(send_back, t)
        if t == TICKS - 1:
            drain()
        both(settle, t)

    for g in range(2):
        for f in range(PARTS):
            for i in range(1, XS):
                b_copy(1, g, i, f).wait_send()
    for g in range(2):
        for f in range(PARTS):
            out_copy(g, f).wait()


def shards(pipes, up_state, down_state, enter_up, enter_down, up_route, down_route, gain, router, w_gate, w_up, w_down):
    features = up_state.shape[2]
    hid = w_down.shape[1]
    vmem = pl.BlockSpec(memory_space=pltpu.VMEM)
    hbm = pl.BlockSpec(memory_space=pl.ANY)
    dma = pltpu.SemaphoreType.DMA
    width = features // PARTS
    out = pl.pallas_call(
        functools.partial(kernel, pipes),
        out_shape=jax.ShapeDtypeStruct((2, ROWS, features), BF16),
        in_specs=[hbm] * 4 + [vmem] * 4 + [hbm] * 3,
        out_specs=hbm,
        scratch_shapes=[
            pltpu.VMEM((features, 4 * hid), BF16),
            pltpu.VMEM((2 * hid, features), BF16),
            pltpu.VMEM((TICKS, 2, PARTS, ROWS, width), BF16),
            pltpu.VMEM((2, PARTS, ROWS, width), BF16),
            pltpu.VMEM((TICKS, 2, PARTS, XS, SUB, width // 2), BF16),
            pltpu.VMEM((TICKS, 2, PARTS, XS, SUB, width // 2), BF16),
            pltpu.VMEM((TICKS, 2, PARTS, SUB, width), BF16),
            pltpu.VMEM((TICKS, 2, PARTS, YS, SUB, width), BF16),
            pltpu.VMEM((TICKS, 2, 2, PARTS, SUB, width), BF16),
            pltpu.VMEM((2, PARTS, YS, SUB, width), F32),
            pltpu.VMEM((TICKS, 2, 2, PARTS, REACH, SUB, width), BF16),
            pltpu.VMEM((TICKS, 2, 2, PARTS, REACH + 1, SUB, width), BF16),
            pltpu.VMEM((TICKS, 2, PARTS, XS, SUB, width // 2), BF16),
            pltpu.VMEM((TICKS, 2, PARTS, XS, SUB, width // 2), BF16),
            pltpu.VMEM((2, PARTS, ROWS, width), BF16),
            pltpu.VMEM((2, 2, ROWS, 128), F32),
            pltpu.VMEM((2, 2, ROWS, 128), F32),
            pltpu.VMEM((2, PARTS, ROWS, width), BF16),
            dma((3,)),
            dma((3,)),
            dma((3,)),
            dma((2, 2, PARTS)),
            dma((2, PARTS)),
            dma((TICKS, 2, XS, PARTS)),
            dma((TICKS, 2, XS, PARTS)),
            dma((TICKS, 2, 2, TRANSIT + 1, PARTS)),
            dma((TICKS, 2, 2, TRANSIT + 1, PARTS)),
            dma((TICKS, 2, 2, TRANSIT + 1, PARTS)),
            dma((TICKS, 2, 2, TRANSIT + 1, PARTS)),
            dma((TICKS, 2, XS, PARTS)),
            dma((TICKS, 2, XS, PARTS)),
            dma((2, 2)),
            dma((2, 2)),
        ],
        compiler_params=pltpu.CompilerParams(
            collective_id=0, has_side_effects=True, vmem_limit_bytes=56 * 1024 * 1024
        ),
    )(
        up_state[0], down_state[0], enter_up, enter_down,
        up_route.reshape(TICKS, ROWS), down_route.reshape(TICKS, ROWS),
        gain, router[0].T, w_gate[0], w_up[0], w_down[0],
    )
    return out[:1], out[1:]


def solution(mesh):
    return jax.shard_map(
        functools.partial(shards, mesh.shape["pipe"]),
        mesh=mesh,
        in_specs=(
            P("pipe", "expert", None),
            P("pipe", "expert", None),
            P("expert", None),
            P("expert", None),
            P(None, "pipe", "expert", None),
            P(None, "pipe", "expert", None),
            P("pipe", None),
            P("pipe", None, None),
            P("pipe", None, "expert"),
            P("pipe", None, "expert"),
            P("pipe", "expert", None),
        ),
        out_specs=(P("pipe", "expert", None), P("pipe", "expert", None)),
        check_vma=False,
    )
```
